32 devices in a mesh: frames: 8 (over y, x, core), planes: 4 (over z).
Axes of the slice: x: 2, y: 2, z: 4, core: 2. Of those that a mesh axis runs over, the one named last changes fastest.
Arguments:
- recording: float32 [64, 4, 256, 128], P('frames', 'planes'), may hold values from -30 to 30
- template: float32 [4, 256, 128], P('planes'), may hold values from -4 to 4
- shifts: int32 [64, 4, 2], P('frames', 'planes'), may hold values from -16 to 16
- support: int32 [256, 48], replicated, may hold values from 0 to 127, as said below
- temporal_init: float32 [64, 256], replicated, may hold values from 0 to 0.3
- spatial_init: float32 [256, 4, 32768], P(None, 'planes', 'frames'), may hold values from 0 to 29
Outputs:
- temporal: float32 [64, 256], replicated
- spatial: float32 [256, 4, 32768], P(None, 'planes', 'frames')
The draws below stay inside these ranges and needn't reach their ends.
Inputs may be any that keep to these rules, and one draw needn't show every extreme that they name: `support`: each component names 48 different tiles.
All inputs are finite; a program needn't handle non-finite values.
Results may differ from the reference program's by a relative error of at most 0.0001.
Values sent between devices are 32-bit elements; how exact they have to be, the bound alone decides.
A program may use at most 128 MiB of HBM per device.

```python
import jax
import jax.numpy as jnp
from jax import lax

HEIGHT = 256
WIDTH = 128
COMP = 256
TILE = 1024
NTREND = 16
ITERS = 1
MAXS = 16
PLANES = 4
FRAMES = 64
TILES = 128
NSUP = 48


def shared_parts(key):
    template_key = jax.random.fold_in(key, 11)
    shift_key = jax.random.fold_in(key, 12)
    template = jnp.clip(jax.random.normal(template_key, (PLANES, HEIGHT, WIDTH), jnp.float32), -4.0, 4.0)
    shifts = jax.random.randint(shift_key, (FRAMES, PLANES, 2), -MAXS, MAXS + 1).astype(jnp.int32)
    return (template, shifts)


def bright_pixels(key):
    picks = jax.random.uniform(jax.random.fold_in(key, 16), (PLANES, HEIGHT, WIDTH), jnp.float32, 0.0, 1.0)
    gain = jnp.where(picks < 0.01, 10.0, 1.0)
    return gain.astype(jnp.float32)


def place_template(picture, offsets):
    return jnp.roll(picture, (-offsets[0], -offsets[1]), axis=(0, 1))


def draw_template(key, part):
    template, shifts = shared_parts(key)
    return template


def draw_shifts(key, part):
    template, shifts = shared_parts(key)
    return shifts


def draw_recording(key, part):
    template, shifts = shared_parts(key)
    data_gain = 1.0 + 0.25 * (bright_pixels(key) - 1.0)
    amplitude = jax.random.uniform(jax.random.fold_in(key, 13), (FRAMES,), jnp.float32, 0.2, 1.5)
    levels = jnp.arange(PLANES).astype(jnp.float32) / max(PLANES - 1, 1)
    brightness = jnp.power(3.0, levels)
    noise_key = jax.random.fold_in(key, 14)
    noise = jnp.clip(jax.random.normal(noise_key, (FRAMES, PLANES, HEIGHT, WIDTH), jnp.float32), -4.0, 4.0)
    placed = jax.vmap(lambda offsets: jax.vmap(place_template)(template, offsets))(shifts)
    placed_gain = jax.vmap(lambda offsets: jax.vmap(place_template)(data_gain, offsets))(shifts)
    movie = brightness[None, :, None, None] * placed_gain * (amplitude[:, None, None, None] * placed + noise)
    return jnp.clip(movie, -30.0, 30.0).astype(jnp.float32)


def draw_spatial_init(key, part):
    gain = bright_pixels(key).reshape(PLANES, HEIGHT * WIDTH)
    factor_key = jax.random.fold_in(key, 17)
    comp_level = jnp.exp(jax.random.uniform(jax.random.fold_in(factor_key, 1), (COMP,), jnp.float32, jnp.log(0.3), jnp.log(3.0)))
    tile_level = jax.random.uniform(jax.random.fold_in(factor_key, 2), (COMP, PLANES, HEIGHT * WIDTH // TILE), jnp.float32, 0.5, 1.5)
    tile_level = jnp.repeat(tile_level, TILE, axis=2)
    pixel_level = jnp.exp(jax.random.uniform(jax.random.fold_in(factor_key, 3), (PLANES, HEIGHT * WIDTH), jnp.float32, 0.0, jnp.log(4.0)))
    base_key = jax.random.fold_in(factor_key, 4)
    base = jax.random.uniform(base_key, (COMP, PLANES, HEIGHT * WIDTH), jnp.float32, 0.0, 0.1)
    values = base * comp_level[:, None, None] * tile_level * (pixel_level * gain)[None]
    return values.astype(jnp.float32)


def pick_tiles(component_key):
    scores = jax.random.randint(component_key, (TILES,), 0, 1 << 20) * TILES + jnp.arange(TILES)
    values, indices = jax.lax.top_k(scores, NSUP)
    return indices.astype(jnp.int32)


def draw_support(key, part):
    component_keys = jax.random.split(jax.random.fold_in(key, 15), COMP)
    return jax.vmap(pick_tiles)(component_keys)


def setup_inputs(seed: int = 0) -> dict:
    streams_of = jax.random.split(jax.random.key(seed), 7)
    return {
        "recording": draw_recording(jax.random.fold_in(streams_of[6], 71), 0),
        "template": draw_template(jax.random.fold_in(streams_of[6], 71), 0),
        "shifts": draw_shifts(jax.random.fold_in(streams_of[6], 71), 0),
        "support": draw_support(jax.random.fold_in(streams_of[6], 71), 0),
        "temporal_init": jnp.clip(jax.random.uniform(streams_of[4], (FRAMES, COMP), jnp.float32, 0.0, 0.3), 0.0, 0.3),
        "spatial_init": draw_spatial_init(jax.random.fold_in(streams_of[6], 71), 0),
    }


epsilon = 1e-06

def matmul(left_side, right_side):
    return jnp.dot(left_side, right_side, precision=lax.Precision.HIGHEST, preferred_element_type=jnp.float32)

def cosine_table(frame_count, basis_order):
    times = jnp.arange(frame_count).astype(jnp.float32)
    orders = jnp.arange(basis_order).astype(jnp.float32)
    scales = jnp.where(orders == 0, jnp.sqrt(1.0 / frame_count), jnp.sqrt(2.0 / frame_count)).astype(jnp.float32)
    return (jnp.cos(jnp.pi * (times[:, None] + 0.5) * orders[None, :] / frame_count) * scales[None, :]).astype(jnp.float32)

def shift_frame(picture, offsets):
    return jnp.roll(picture, (offsets[0], offsets[1]), axis=(0, 1))

def reference(recording, template, shifts, support, temporal_init, spatial_init):
    registered = jax.vmap(jax.vmap(shift_frame))(recording, shifts)
    numerator = lax.optimization_barrier(jnp.sum(registered * template[None], axis=(1, 2, 3)))
    energy = lax.optimization_barrier(jnp.sum(registered * registered, axis=(1, 2, 3)))
    template_energy = jnp.sum(template * template)
    weight = numerator / jnp.sqrt(energy * template_energy + epsilon)
    series = (registered * weight[:, None, None, None]).reshape(FRAMES, PLANES * HEIGHT * WIDTH)
    cosine_basis = cosine_table(FRAMES, NTREND)
    detrended = series - matmul(cosine_basis, matmul(cosine_basis.T, series))
    tile_ids = jnp.arange(TILES).astype(jnp.int32)
    covered = jnp.any(support[:, :, None] == tile_ids[None, None, :], axis=1).astype(jnp.float32)
    support_mask = jnp.repeat(covered, TILE, axis=1)
    spatial = spatial_init.reshape(COMP, PLANES * HEIGHT * WIDTH) * support_mask
    temporal = temporal_init
    for iteration in range(ITERS):
        spatial_gram = matmul(spatial, spatial.T)
        cross = matmul(detrended, spatial.T)
        temporal_grad = matmul(temporal, spatial_gram) - cross
        grad_square = jnp.sum(temporal_grad * temporal_grad)
        grad_curve = jnp.sum(temporal_grad * matmul(temporal_grad, spatial_gram))
        temporal = jnp.maximum(temporal - grad_square / (grad_curve + epsilon) * temporal_grad, 0.0)
        temporal_gram = matmul(temporal.T, temporal)
        spatial_grad = (matmul(temporal_gram, spatial) - matmul(temporal.T, detrended)) * support_mask
        grad_square = jnp.sum(spatial_grad * spatial_grad)
        grad_curve = jnp.sum(spatial_grad * matmul(temporal_gram, spatial_grad))
        spatial = jnp.maximum(spatial - grad_square / (grad_curve + epsilon) * spatial_grad, 0.0)
    return (temporal, spatial.reshape(COMP, PLANES, HEIGHT * WIDTH))
```

```python
import functools

import jax
import jax.numpy as jnp
import numpy as np
from jax import lax
from jax.experimental import pallas as pl
from jax.experimental.pallas import tpu as pltpu
from jax.sharding import PartitionSpec as P

TILE = 1024
NTREND = 16
LANES = 128
SUBS = 8
MESH = pl.DeviceIdType.MESH
F32 = jnp.float32
BF16 = jnp.bfloat16
HIGH = lax.Precision.HIGH
HIGHEST = lax.Precision.HIGHEST

epsilon = 1e-06

NN = (((1,), (0,)), ((), ()))
NT = (((1,), (1,)), ((), ()))


def trend_projection(frame_count, basis_order):
    times = np.arange(frame_count) + 0.5
    orders = np.arange(basis_order)
    scales = np.where(orders == 0, np.sqrt(1.0 / frame_count), np.sqrt(2.0 / frame_count))
    basis = np.cos(np.pi * times[:, None] * orders[None, :] / frame_count) * scales[None, :]
    return (np.eye(frame_count) - basis @ basis.T).astype(np.float32)


def split(x):
    high = x.astype(BF16)
    return high, (x - high.astype(F32)).astype(BF16)


def dot1(a, b, dims=NN):
    return lax.dot_general(a, b, dims, preferred_element_type=F32)


def dot3(a, b, dims=NN):
    return dot1(a[0], b[0], dims) + (dot1(a[0], b[1], dims) + dot1(a[1], b[0], dims))


def fold(x):
    rows, columns = x.shape
    line = x[:, :LANES]
    for j in range(1, columns // LANES):
        line = line + x[:, j * LANES : (j + 1) * LANES]
    return jnp.sum(line.reshape(rows // SUBS, SUBS, LANES), axis=0)


def total(x):
    return jnp.sum(jnp.sum(x, axis=0, keepdims=True), axis=1, keepdims=True)


def register_kernel(shifts_ref, rec_ref, tmpl_ref, payload_ref, stats_ref, reg_ref):
    frames, height, width = rec_ref.shape
    tmpl = tmpl_ref[...]
    for f in range(frames):
        x = rec_ref[f]
        across = lax.rem(shifts_ref[f, 1] + width, width)
        down = lax.rem(shifts_ref[f, 0] + height, height)
        y = pltpu.roll(pltpu.roll(x, across, 1), down, 0)
        reg_ref[f * height : (f + 1) * height, :] = y
        stats_ref[f : f + 1, :] = jnp.sum(y * tmpl, axis=0, keepdims=True)
        stats_ref[frames + f : frames + f + 1, :] = jnp.sum(x * x, axis=0, keepdims=True)
    stats_ref[2 * frames :, :] = fold(tmpl * tmpl)
    for r in range(height):
        payload_ref[:, r * width : (r + 1) * width] = reg_ref[pl.ds(r, frames, stride=height), :]


def main_kernel(
    nf, nz, pixel_count,
    payload_ref, stats_ref, support_ref, proj_ref, w0_ref, h0_ref,
    temporal_ref, scal_ref, g_out, hm_out,
    hf, hhi, hlo, gbuf, rbuf, dbuf, cov, gram, gramx, wcol, zbuf,
    stz, stf, tgl, rs, tz, tgf, qz, qf, gz, gf, sems, lsem,
):
    f = lax.axis_index("frames")
    z = lax.axis_index("planes")
    comps, pixels = hf.shape
    total_frames = w0_ref.shape[0]
    fl = total_frames // nf
    tiles = pixels // TILE
    own = pl.ds(pl.multiple_of(f * fl, fl), fl)

    def over_frames(k, source, target):
        copies = []
        for d in range(1, nf):
            peer = lax.rem(f + d, nf)
            copies.append(
                pltpu.make_async_remote_copy(
                    src_ref=source(peer), dst_ref=target,
                    send_sem=sems.at[k, 0, d], recv_sem=sems.at[k, 1, d],
                    device_id=(peer, z), device_id_type=MESH,
                )
            )
        for copy in copies:
            copy.start()
        return copies

    def over_planes(k, source, target):
        copies = []
        for d in range(1, nz):
            peer = lax.rem(z + d, nz)
            copies.append(
                pltpu.make_async_remote_copy(
                    src_ref=source, dst_ref=target,
                    send_sem=sems.at[k, 0, d], recv_sem=sems.at[k, 1, d],
                    device_id=(f, peer), device_id_type=MESH,
                )
            )
        for copy in copies:
            copy.start()
        return copies

    def wait(copies):
        for copy in copies:
            copy.wait()

    load_h = pltpu.make_async_copy(h0_ref, hf, lsem.at[0])
    load_h.start()
    mine = pltpu.make_async_copy(
        payload_ref.at[:, pl.ds(pl.multiple_of(f * pixels, pixels), pixels)],
        rbuf.at[own, :], lsem.at[1],
    )
    mine.start()

    barrier = pltpu.get_barrier_semaphore()
    for d in range(1, nf):
        pl.semaphore_signal(barrier, inc=1, device_id=(lax.rem(f + d, nf), z), device_id_type=MESH)
    for d in range(1, nz):
        pl.semaphore_signal(barrier, inc=1, device_id=(f, lax.rem(z + d, nz)), device_id_type=MESH)
    pl.semaphore_wait(barrier, nf - 1 + nz - 1)

    stz[z] = stats_ref[...]
    plane_stats = over_planes(0, stats_ref, stz.at[z])
    pixel_copies = over_frames(
        1,
        lambda peer: payload_ref.at[:, pl.ds(pl.multiple_of(peer * pixels, pixels), pixels)],
        rbuf.at[own, :],
    )

    wait(plane_stats)
    summed = stz[0]
    for i in range(1, nz):
        summed = summed + stz[i]
    stf[f] = summed
    frame_stats = over_frames(2, lambda peer: stf.at[f], stf.at[f])

    load_h.wait()
    gram[...] = jnp.zeros_like(gram)
    gramx[...] = jnp.zeros_like(gramx)
    first_tile = z * (pixel_count // TILE) + f * tiles

    def prepare(c, carry):
        columns = pl.ds(pl.multiple_of(c * TILE, TILE), TILE)
        hit = jnp.where(support_ref[...] == first_tile + c, 1.0, 0.0).astype(F32)
        covered = jnp.broadcast_to(jnp.max(hit, axis=1, keepdims=True), (comps, LANES))
        cov[c] = covered
        h = hf[:, columns] * jnp.concatenate([covered] * (TILE // LANES), axis=1)
        hf[:, columns] = h
        high, low = split(h)
        hhi[:, columns] = high
        hlo[:, columns] = low
        gram[...] += dot1(high, high, NT)
        gramx[...] += dot1(high, low, NT)
        return carry

    lax.fori_loop(0, tiles, prepare, 0)
    save_h = pltpu.make_async_copy(hf, hm_out, lsem.at[2])
    save_h.start()
    gram[...] += gramx[...] + gramx[...].T
    w0 = w0_ref[...]
    tgl[...] = jnp.dot(w0, gram[...], precision=HIGHEST, preferred_element_type=F32)

    wait(frame_stats)
    template_energy = total(summed[2 * fl :, :])
    for s in range(nf):
        sums = stf[s]
        numerator = jnp.sum(sums[:fl], axis=1, keepdims=True)
        energy = jnp.sum(sums[fl : 2 * fl], axis=1, keepdims=True)
        weight = numerator / jnp.sqrt(energy * template_energy + epsilon)
        wcol[s * fl : (s + 1) * fl, :] = jnp.broadcast_to(weight, (fl, LANES))

    mine.wait()
    wait(pixel_copies)
    zbuf[...] = jnp.zeros_like(zbuf)

    def correlate(c, carry):
        columns = pl.ds(pl.multiple_of(c * TILE, TILE), TILE)
        series = rbuf[:, columns] * jnp.concatenate([wcol[...]] * (TILE // LANES), axis=1)
        rbuf[:, columns] = series
        zbuf[...] += dot3(split(series), (hhi[:, columns], hlo[:, columns]), NT)
        return carry

    lax.fori_loop(0, tiles, correlate, 0)
    tgl[...] -= jnp.dot(proj_ref[...], zbuf[...], precision=HIGHEST, preferred_element_type=F32)

    rs[f] = tgl[own, :]
    scatter = over_frames(
        3, lambda peer: tgl.at[pl.ds(pl.multiple_of(peer * fl, fl), fl), :], rs.at[f]
    )

    def detrend(c, carry):
        columns = pl.ds(pl.multiple_of(c * TILE, TILE), TILE)
        dbuf[:, columns] = dot3(split(proj_ref[...]), split(rbuf[:, columns]))
        return carry

    lax.fori_loop(0, tiles, detrend, 0)
    wait(scatter)
    part = rs[0]
    for i in range(1, nf):
        part = part + rs[i]
    tz[z] = part
    wait(over_planes(4, tz.at[z], tz.at[z]))
    part = tz[0]
    for i in range(1, nz):
        part = part + tz[i]
    tgf[own, :] = part
    wait(over_frames(5, lambda peer: tgf.at[own, :], tgf.at[own, :]))

    def all_sum(k, value, planes_buf, frames_buf):
        planes_buf[z] = value
        wait(over_planes(k, planes_buf.at[z], planes_buf.at[z]))
        value = planes_buf[0]
        for i in range(1, nz):
            value = value + planes_buf[i]
        frames_buf[f] = value
        wait(over_frames(k + 1, lambda peer: frames_buf.at[f], frames_buf.at[f]))
        value = frames_buf[0]
        for i in range(1, nf):
            value = value + frames_buf[i]
        return value

    grad = tgf[...]
    curve = fold(grad * jnp.dot(grad, gram[...], precision=HIGHEST, preferred_element_type=F32))
    curve = total(all_sum(6, curve, qz, qf))
    step = total(fold(grad * grad)) / (curve + epsilon)
    w1 = jnp.maximum(w0 - step * grad, 0.0)
    temporal_ref[...] = w1
    w1s = split(w1)
    w1t = split(w1.T)

    def gradient(c, carry):
        squares, curves = carry
        columns = pl.ds(pl.multiple_of(c * TILE, TILE), TILE)
        error = dot3(w1s, (hhi[:, columns], hlo[:, columns])) - dbuf[:, columns]
        g = dot3(w1t, split(error)) * jnp.concatenate([cov[c]] * (TILE // LANES), axis=1)
        gbuf[:, columns] = g
        bent = dot3(w1s, split(g))
        return squares + fold(g * g), curves + fold(bent * bent)

    nothing = jnp.zeros((SUBS, LANES), F32)
    squares, curves = lax.fori_loop(0, tiles, gradient, (nothing, nothing))
    save_g = pltpu.make_async_copy(gbuf, g_out, lsem.at[3])
    save_g.start()
    sums = all_sum(8, jnp.concatenate([squares, curves], axis=0), gz, gf)
    step = total(sums[:SUBS]) / (total(sums[SUBS:]) + epsilon)
    scal_ref[...] = jnp.broadcast_to(step, (SUBS, LANES))
    save_h.wait()
    save_g.wait()


def body(nf, nz, recording, template, shifts, support, temporal_init, spatial_init):
    frames, planes, height, width = recording.shape
    comps = spatial_init.shape[0]
    pixels = spatial_init.shape[1] * spatial_init.shape[2]
    pixel_count = height * width
    total_frames = temporal_init.shape[0]
    tiles = pixels // TILE
    vmem = pl.BlockSpec(memory_space=pltpu.VMEM)
    hbm = pl.BlockSpec(memory_space=pl.ANY)
    payload, stats = pl.pallas_call(
        register_kernel,
        out_shape=(
            jax.ShapeDtypeStruct((frames, pixel_count), F32),
            jax.ShapeDtypeStruct((2 * frames + SUBS, LANES), F32),
        ),
        in_specs=[pl.BlockSpec(memory_space=pltpu.SMEM), vmem, vmem],
        out_specs=(vmem, vmem),
        scratch_shapes=[pltpu.VMEM((frames * height, width), F32)],
        name="register",
    )(
        shifts.reshape(frames, 2),
        recording.reshape(frames, height, width),
        template.reshape(height, width),
    )
    count = max(nf, nz)
    temporal, scal, grad, masked = pl.pallas_call(
        functools.partial(main_kernel, nf, nz, pixel_count),
        out_shape=(
            jax.ShapeDtypeStruct((total_frames, comps), F32),
            jax.ShapeDtypeStruct((SUBS, LANES), F32),
            jax.ShapeDtypeStruct((comps, pixels), F32),
            jax.ShapeDtypeStruct((comps, pixels), F32),
        ),
        in_specs=[hbm, vmem, vmem, vmem, vmem, hbm],
        out_specs=(vmem, vmem, hbm, hbm),
        scratch_shapes=[
            pltpu.VMEM((comps, pixels), F32),
            pltpu.VMEM((comps, pixels), BF16),
            pltpu.VMEM((comps, pixels), BF16),
            pltpu.VMEM((comps, pixels), F32),
            pltpu.VMEM((total_frames, pixels), F32),
            pltpu.VMEM((total_frames, pixels), F32),
            pltpu.VMEM((tiles, comps, LANES), F32),
            pltpu.VMEM((comps, comps), F32),
            pltpu.VMEM((comps, comps), F32),
            pltpu.VMEM((total_frames, LANES), F32),
            pltpu.VMEM((total_frames, comps), F32),
            pltpu.VMEM((nz, 2 * frames + SUBS, LANES), F32),
            pltpu.VMEM((nf, 2 * frames + SUBS, LANES), F32),
            pltpu.VMEM((total_frames, comps), F32),
            pltpu.VMEM((nf, frames, comps), F32),
            pltpu.VMEM((nz, frames, comps), F32),
            pltpu.VMEM((total_frames, comps), F32),
            pltpu.VMEM((nz, SUBS, LANES), F32),
            pltpu.VMEM((nf, SUBS, LANES), F32),
            pltpu.VMEM((nz, 2 * SUBS, LANES), F32),
            pltpu.VMEM((nf, 2 * SUBS, LANES), F32),
            pltpu.SemaphoreType.DMA((10, 2, count)),
            pltpu.SemaphoreType.DMA((4,)),
        ],
        compiler_params=pltpu.CompilerParams(
            collective_id=0, has_side_effects=True, vmem_limit_bytes=40 * 1024 * 1024
        ),
        name="factorize",
    )(
        payload,
        stats,
        support,
        jnp.asarray(trend_projection(total_frames, NTREND)),
        temporal_init,
        spatial_init.reshape(comps, pixels),
    )
    spatial = jnp.maximum(masked - scal[0, 0] * grad, 0.0)
    return temporal, spatial.reshape(spatial_init.shape)


def solution(mesh):
    placed = (
        P("frames", "planes", None, None),
        P("planes", None, None),
        P("frames", "planes", None),
        P(),
        P(),
        P(None, "planes", "frames"),
    )
    return jax.shard_map(
        functools.partial(body, mesh.shape["frames"], mesh.shape["planes"]),
        mesh=mesh,
        in_specs=placed,
        out_specs=(P(), P(None, "planes", "frames")),
        check_vma=False,
    )
```

```python
import functools

import jax
import jax.numpy as jnp
import numpy as np
from jax import lax
from jax.experimental import pallas as pl
from jax.experimental.pallas import tpu as pltpu
from jax.sharding import PartitionSpec as P

TILE = 1024
NTREND = 16
LANES = 128
SUBS = 8
FINISH = 8
MESH = pl.DeviceIdType.MESH
F32 = jnp.float32
BF16 = jnp.bfloat16
HIGH = lax.Precision.HIGH
HIGHEST = lax.Precision.HIGHEST

epsilon = 1e-06

NN = (((1,), (0,)), ((), ()))
NT = (((1,), (1,)), ((), ()))


def trend_projection(frame_count, basis_order):
    times = np.arange(frame_count) + 0.5
    orders = np.arange(basis_order)
    scales = np.where(orders == 0, np.sqrt(1.0 / frame_count), np.sqrt(2.0 / frame_count))
    basis = np.cos(np.pi * times[:, None] * orders[None, :] / frame_count) * scales[None, :]
    return (np.eye(frame_count) - basis @ basis.T).astype(np.float32)


def split(x):
    high = x.astype(BF16)
    return high, (x - high.astype(F32)).astype(BF16)


def dot1(a, b, dims=NN):
    return lax.dot_general(a, b, dims, preferred_element_type=F32)


def stack(a):
    return jnp.concatenate(a, axis=0)


def dot_rows(stacked, high, low, dims=NN):
    rows = stacked.shape[0] // 2
    first = dot1(stacked, high, dims)
    first = first[:rows] + first[rows:]
    if low is None:
        return first
    return first + dot1(stacked[:rows], low, dims)


def deep_left(x):
    high, low = split(x)
    return jnp.concatenate([high, low, high], axis=1)


def deep_right(x):
    high, low = split(x)
    return jnp.concatenate([high, high, low], axis=0)


def fold(x):
    rows, columns = x.shape
    line = x[:, :LANES]
    for j in range(1, columns // LANES):
        line = line + x[:, j * LANES : (j + 1) * LANES]
    return jnp.sum(line.reshape(rows // SUBS, SUBS, LANES), axis=0)


def total(x):
    return jnp.sum(jnp.sum(x, axis=0, keepdims=True), axis=1, keepdims=True)


def register_kernel(shifts_ref, rec_ref, tmpl_ref, payload_ref, stats_ref, reg_ref):
    frames, height, width = rec_ref.shape
    tmpl = tmpl_ref[...]
    for f in range(frames):
        x = rec_ref[f]
        across = lax.rem(shifts_ref[1, f] + width, width)
        down = lax.rem(shifts_ref[0, f] + height, height)
        y = pltpu.roll(pltpu.roll(x, across, 1), down, 0)
        reg_ref[f * height : (f + 1) * height, :] = y
        stats_ref[f : f + 1, :] = jnp.sum(y * tmpl, axis=0, keepdims=True)
        stats_ref[frames + f : frames + f + 1, :] = jnp.sum(x * x, axis=0, keepdims=True)
    stats_ref[2 * frames :, :] = fold(tmpl * tmpl)
    for r in range(height):
        payload_ref[:, r * width : (r + 1) * width] = reg_ref[pl.ds(r, frames, stride=height), :]


def main_kernel(
    nf, nz, pixel_count,
    payload_ref, stats_ref, support_ref, proj_ref, w0_ref, h0_ref,
    temporal_ref, scal_ref, gbuf, hf,
    hraw, hhi, hlo, rbuf, dbuf, cov, gram, gramx, wcol, zbuf,
    stz, stf, tgl, rs, tz, tgf, qz, qf, gz, gf, sems, lsem,
):
    f = lax.axis_index("frames")
    z = lax.axis_index("planes")
    comps, pixels = hf.shape
    total_frames = w0_ref.shape[0]
    fl = total_frames // nf
    tiles = pixels // TILE
    own = pl.ds(pl.multiple_of(f * fl, fl), fl)

    def over_frames(k, source, target):
        copies = []
        for d in range(1, nf):
            peer = lax.rem(f + d, nf)
            copies.append(
                pltpu.make_async_remote_copy(
                    src_ref=source(peer), dst_ref=target,
                    send_sem=sems.at[k, 0, d], recv_sem=sems.at[k, 1, d],
                    device_id=(peer, z), device_id_type=MESH,
                )
            )
        for copy in copies:
            copy.start()
        return copies

    def over_planes(k, source, target):
        copies = []
        for d in range(1, nz):
            peer = lax.rem(z + d, nz)
            copies.append(
                pltpu.make_async_remote_copy(
                    src_ref=source, dst_ref=target,
                    send_sem=sems.at[k, 0, d], recv_sem=sems.at[k, 1, d],
                    device_id=(f, peer), device_id_type=MESH,
                )
            )
        for copy in copies:
            copy.start()
        return copies

    def wait(copies):
        for copy in copies:
            copy.wait()

    load_h = pltpu.make_async_copy(h0_ref, hraw, lsem.at[0])
    load_h.start()
    def part_of(device, c):
        return pl.ds(pl.multiple_of(device * pixels + c * TILE, TILE), TILE)

    mine = []
    for c in range(tiles):
        columns = pl.ds(c * TILE, TILE)
        copy = pltpu.make_async_copy(
            payload_ref.at[:, part_of(f, c)], rbuf.at[own, columns], lsem.at[1 + c]
        )
        copy.start()
        mine.append(copy)

    barrier = pltpu.get_barrier_semaphore()
    for d in range(1, nf):
        pl.semaphore_signal(barrier, inc=1, device_id=(lax.rem(f + d, nf), z), device_id_type=MESH)
    for d in range(1, nz):
        pl.semaphore_signal(barrier, inc=1, device_id=(f, lax.rem(z + d, nz)), device_id_type=MESH)
    pl.semaphore_wait(barrier, nf - 1 + nz - 1)

    stz[z] = stats_ref[...]
    plane_stats = over_planes(0, stats_ref, stz.at[z])
    pixel_copies = [
        over_frames(
            9 + c,
            lambda peer, c=c: payload_ref.at[:, part_of(peer, c)],
            rbuf.at[own, pl.ds(c * TILE, TILE)],
        )
        for c in range(tiles)
    ]

    wait(plane_stats)
    summed = stz[0]
    for i in range(1, nz):
        summed = summed + stz[i]
    stf[f] = summed
    frame_stats = over_frames(1, lambda peer: stf.at[f], stf.at[f])

    load_h.wait()
    gram[...] = jnp.zeros_like(gram)
    gramx[...] = jnp.zeros_like(gramx)
    first_tile = z * (pixel_count // TILE) + f * tiles

    def prepare(c, carry):
        hit = jnp.where(support_ref[...] == first_tile + c, 1.0, 0.0).astype(F32)
        row = jnp.max(hit, axis=0, keepdims=True)
        covered = jnp.broadcast_to(row, (LANES, comps)).T
        cov[c] = covered
        for j in range(TILE // LANES):
            columns = pl.ds(pl.multiple_of(c * TILE + j * LANES, LANES), LANES)
            lines = pl.ds(c * (TILE // LANES) + j, comps, stride=pixels // LANES)
            h = hraw[lines, :] * covered
            hf[:, columns] = h
            high, low = split(h)
            hhi[:, columns] = high
            hlo[:, columns] = low
        columns = pl.ds(pl.multiple_of(c * TILE, TILE), TILE)
        both = jnp.concatenate([hhi[:, columns], hlo[:, columns]], axis=0)
        product = dot1(both, hhi[:, columns], NT)
        gram[...] += product[:comps]
        gramx[...] += product[comps:]
        return carry

    lax.fori_loop(0, tiles, prepare, 0)
    gram[...] += gramx[...] + gramx[...].T
    w0 = w0_ref[...]
    tgl[...] = jnp.dot(w0, gram[...], precision=HIGHEST, preferred_element_type=F32)

    wait(frame_stats)
    template_energy = total(summed[2 * fl :, :])
    for s in range(nf):
        sums = stf[s]
        numerator = jnp.sum(sums[:fl], axis=1, keepdims=True)
        energy = jnp.sum(sums[fl : 2 * fl], axis=1, keepdims=True)
        weight = numerator / jnp.sqrt(energy * template_energy + epsilon)
        wcol[s * fl : (s + 1) * fl, :] = jnp.broadcast_to(weight, (fl, LANES))

    zbuf[...] = jnp.zeros_like(zbuf)
    for c in range(tiles):
        mine[c].wait()
        wait(pixel_copies[c])
        columns = pl.ds(c * TILE, TILE)
        series = rbuf[:, columns] * jnp.concatenate([wcol[...]] * (TILE // LANES), axis=1)
        rbuf[:, columns] = series
        zbuf[...] += dot_rows(stack(split(series)), hhi[:, columns], hlo[:, columns], NT)

    tgl[...] -= jnp.dot(proj_ref[...], zbuf[...], precision=HIGHEST, preferred_element_type=F32)

    rs[f] = tgl[own, :]
    scatter = over_frames(
        2, lambda peer: tgl.at[pl.ds(pl.multiple_of(peer * fl, fl), fl), :], rs.at[f]
    )

    proj = deep_left(proj_ref[...])

    def detrend(c, carry):
        columns = pl.ds(pl.multiple_of(c * TILE, TILE), TILE)
        dbuf[:, columns] = dot1(proj, deep_right(rbuf[:, columns]))
        return carry

    lax.fori_loop(0, tiles, detrend, 0)
    wait(scatter)
    part = rs[0]
    for i in range(1, nf):
        part = part + rs[i]
    tz[z] = part
    wait(over_planes(3, tz.at[z], tz.at[z]))
    part = tz[0]
    for i in range(1, nz):
        part = part + tz[i]
    tgf[own, :] = part
    wait(over_frames(4, lambda peer: tgf.at[own, :], tgf.at[own, :]))

    def all_sum(k, value, planes_buf, frames_buf):
        planes_buf[z] = value
        wait(over_planes(k, planes_buf.at[z], planes_buf.at[z]))
        value = planes_buf[0]
        for i in range(1, nz):
            value = value + planes_buf[i]
        frames_buf[f] = value
        wait(over_frames(k + 2, lambda peer: frames_buf.at[f], frames_buf.at[f]))
        value = frames_buf[0]
        for i in range(1, nf):
            value = value + frames_buf[i]
        return value

    grad = tgf[...]
    curve = fold(grad * jnp.dot(grad, gram[...], precision=HIGHEST, preferred_element_type=F32))
    curve = total(all_sum(5, curve, qz, qf))
    step = total(fold(grad * grad)) / (curve + epsilon)
    w1 = jnp.maximum(w0 - step * grad, 0.0)
    temporal_ref[...] = w1
    w1s = stack(split(w1))
    w1t = deep_left(w1.T)

    def gradient(c, carry):
        squares, curves = carry
        columns = pl.ds(pl.multiple_of(c * TILE, TILE), TILE)
        error = dot_rows(w1s, hhi[:, columns], hlo[:, columns]) - dbuf[:, columns]
        g = dot1(w1t, deep_right(error)) * jnp.concatenate([cov[c]] * (TILE // LANES), axis=1)
        gbuf[:, columns] = g
        bent = dot_rows(w1s, g.astype(BF16), None)
        return squares + fold(g * g), curves + fold(bent * bent)

    nothing = jnp.zeros((SUBS, LANES), F32)
    squares, curves = lax.fori_loop(0, tiles, gradient, (nothing, nothing))
    sums = all_sum(6, jnp.concatenate([squares, curves], axis=0), gz, gf)
    step = total(sums[:SUBS]) / (total(sums[SUBS:]) + epsilon)
    scal_ref[...] = jnp.broadcast_to(step, (SUBS, LANES))


def finish_kernel(temporal_ref, scal_ref, g_ref, h_ref, temporal_out, spatial_out, buf, sems):
    comps, pixels = h_ref.shape
    lines = pixels // LANES
    rows = comps // FINISH
    step = jnp.broadcast_to(scal_ref[0:1, :], (rows, LANES))
    first = pltpu.make_async_copy(temporal_ref, temporal_out, sems.at[FINISH])
    first.start()
    copies = []
    for b in range(FINISH):
        for j in range(lines):
            block = (slice(b * rows, (b + 1) * rows), slice(j * LANES, (j + 1) * LANES))
            value = jnp.maximum(h_ref[block] - step * g_ref[block], 0.0)
            buf[pl.ds(b * rows * lines + j, rows, stride=lines), :] = value
        part = pl.ds(b * rows * lines, rows * lines)
        copy = pltpu.make_async_copy(buf.at[part, :], spatial_out.at[part, :], sems.at[b])
        copy.start()
        copies.append(copy)
    first.wait()
    for copy in copies:
        copy.wait()


def body(nf, nz, recording, template, shifts, support, temporal_init, spatial_init):
    frames, planes, height, width = recording.shape
    comps = spatial_init.shape[0]
    pixels = spatial_init.shape[1] * spatial_init.shape[2]
    pixel_count = height * width
    total_frames = temporal_init.shape[0]
    tiles = pixels // TILE
    vmem = pl.BlockSpec(memory_space=pltpu.VMEM)
    hbm = pl.BlockSpec(memory_space=pl.ANY)
    payload, stats = pl.pallas_call(
        register_kernel,
        out_shape=(
            jax.ShapeDtypeStruct((frames, pixel_count), F32),
            jax.ShapeDtypeStruct((2 * frames + SUBS, LANES), F32),
        ),
        in_specs=[pl.BlockSpec(memory_space=pltpu.SMEM), vmem, vmem],
        out_specs=(vmem, vmem),
        scratch_shapes=[pltpu.VMEM((frames * height, width), F32)],
        name="register",
    )(
        shifts.reshape(frames, 2).T,
        recording.reshape(frames, height, width),
        template.reshape(height, width),
    )
    count = max(nf, nz)
    temporal, scal, grad, masked = pl.pallas_call(
        functools.partial(main_kernel, nf, nz, pixel_count),
        out_shape=(
            jax.ShapeDtypeStruct((total_frames, comps), F32),
            jax.ShapeDtypeStruct((SUBS, LANES), F32),
            jax.ShapeDtypeStruct((comps, pixels), F32),
            jax.ShapeDtypeStruct((comps, pixels), F32),
        ),
        in_specs=[hbm, vmem, vmem, vmem, vmem, hbm],
        out_specs=(vmem, vmem, vmem, vmem),
        scratch_shapes=[
            pltpu.VMEM((comps * pixels // LANES, LANES), F32),
            pltpu.VMEM((comps, pixels), BF16),
            pltpu.VMEM((comps, pixels), BF16),
            pltpu.VMEM((total_frames, pixels), F32),
            pltpu.VMEM((total_frames, pixels), F32),
            pltpu.VMEM((tiles, comps, LANES), F32),
            pltpu.VMEM((comps, comps), F32),
            pltpu.VMEM((comps, comps), F32),
            pltpu.VMEM((total_frames, LANES), F32),
            pltpu.VMEM((total_frames, comps), F32),
            pltpu.VMEM((nz, 2 * frames + SUBS, LANES), F32),
            pltpu.VMEM((nf, 2 * frames + SUBS, LANES), F32),
            pltpu.VMEM((total_frames, comps), F32),
            pltpu.VMEM((nf, frames, comps), F32),
            pltpu.VMEM((nz, frames, comps), F32),
            pltpu.VMEM((total_frames, comps), F32),
            pltpu.VMEM((nz, SUBS, LANES), F32),
            pltpu.VMEM((nf, SUBS, LANES), F32),
            pltpu.VMEM((nz, 2 * SUBS, LANES), F32),
            pltpu.VMEM((nf, 2 * SUBS, LANES), F32),
            pltpu.SemaphoreType.DMA((9 + tiles, 2, count)),
            pltpu.SemaphoreType.DMA((1 + tiles,)),
        ],
        compiler_params=pltpu.CompilerParams(
            collective_id=0, has_side_effects=True, vmem_limit_bytes=40 * 1024 * 1024
        ),
        name="factorize",
    )(
        payload,
        stats,
        support.T,
        jnp.asarray(trend_projection(total_frames, NTREND)),
        temporal_init,
        spatial_init.reshape(comps * pixels // LANES, LANES),
    )
    temporal, spatial = pl.pallas_call(
        finish_kernel,
        out_shape=(
            jax.ShapeDtypeStruct((total_frames, comps), F32),
            jax.ShapeDtypeStruct((comps * pixels // LANES, LANES), F32),
        ),
        in_specs=[vmem, vmem, vmem, vmem],
        out_specs=(hbm, hbm),
        scratch_shapes=[
            pltpu.VMEM((comps * pixels // LANES, LANES), F32),
            pltpu.SemaphoreType.DMA((FINISH + 1,)),
        ],
        compiler_params=pltpu.CompilerParams(vmem_limit_bytes=16 * 1024 * 1024),
        name="finish",
    )(temporal, scal, grad, masked)
    return temporal, spatial.reshape(spatial_init.shape)


def solution(mesh):
    placed = (
        P("frames", "planes", None, None),
        P("planes", None, None),
        P("frames", "planes", None),
        P(),
        P(),
        P(None, "planes", "frames"),
    )
    return jax.shard_map(
        functools.partial(body, mesh.shape["frames"], mesh.shape["planes"]),
        mesh=mesh,
        in_specs=placed,
        out_specs=(P(), P(None, "planes", "frames")),
        check_vma=False,
    )
```

```python
import functools

import jax
import jax.numpy as jnp
import numpy as np
from jax import lax
from jax.experimental import pallas as pl
from jax.experimental.pallas import tpu as pltpu
from jax.sharding import PartitionSpec as P

TILE = 1024
NTREND = 16
LANES = 128
SUBS = 8
FINISH = 8
VMEM_LIMIT = 60 * 1000 * 1000
MESH = pl.DeviceIdType.MESH
F32 = jnp.float32
BF16 = jnp.bfloat16

epsilon = 1e-06

NN = (((1,), (0,)), ((), ()))
NT = (((1,), (1,)), ((), ()))


def trend_projection(frame_count, basis_order):
    times = np.arange(frame_count) + 0.5
    orders = np.arange(basis_order)
    scales = np.where(orders == 0, np.sqrt(1.0 / frame_count), np.sqrt(2.0 / frame_count))
    basis = np.cos(np.pi * times[:, None] * orders[None, :] / frame_count) * scales[None, :]
    return (np.eye(frame_count) - basis @ basis.T).astype(np.float32)


def split(x):
    high = x.astype(BF16)
    return high, (x - high.astype(F32)).astype(BF16)


def dot1(a, b, dims=NN):
    return lax.dot_general(a, b, dims, preferred_element_type=F32)


def stack(a):
    return jnp.concatenate(a, axis=0)


def dot_rows(stacked, high, low, dims=NN):
    rows = stacked.shape[0] // 2
    first = dot1(stacked, high, dims)
    first = first[:rows] + first[rows:]
    if low is None:
        return first
    return first + dot1(stacked[:rows], low, dims)


def deep_left(x):
    high, low = split(x)
    return jnp.concatenate([high, low, high], axis=1)


def deep_right(x):
    high, low = split(x)
    return jnp.concatenate([high, high, low], axis=0)


def fold(x):
    rows, columns = x.shape
    line = x[:, :LANES]
    for j in range(1, columns // LANES):
        line = line + x[:, j * LANES : (j + 1) * LANES]
    return jnp.sum(line.reshape(rows // SUBS, SUBS, LANES), axis=0)


def total(x):
    return jnp.sum(jnp.sum(x, axis=0, keepdims=True), axis=1, keepdims=True)


def register(shifts_ref, rec_ref, tmpl_ref, payload_ref, stats_ref, reg_ref):
    frames, height, width = rec_ref.shape
    tmpl = tmpl_ref[...]
    for f in range(frames):
        x = rec_ref[f]
        across = lax.rem(shifts_ref[1, f] + width, width)
        down = lax.rem(shifts_ref[0, f] + height, height)
        y = pltpu.roll(pltpu.roll(x, across, 1), down, 0)
        reg_ref[f * height : (f + 1) * height, :] = y
        stats_ref[f : f + 1, :] = jnp.sum(y * tmpl, axis=0, keepdims=True)
        stats_ref[frames + f : frames + f + 1, :] = jnp.sum(x * x, axis=0, keepdims=True)
    stats_ref[2 * frames :, :] = fold(tmpl * tmpl)
    for r in range(height):
        payload_ref[:, r * width : (r + 1) * width] = reg_ref[pl.ds(r, frames, stride=height), :]


def main_kernel(
    nf, nz, pixel_count,
    shifts_ref, rec_hbm, tmpl_hbm, support_hbm, proj_hbm, w0_hbm, h0_ref,
    temporal_ref, h_out,
    rec_ref, tmpl_ref, support_ref, proj_ref, w0_ref, payload_ref, stats_ref, reg_ref,
    hraw, hhi, hlo, hf, gbuf, rbuf, dbuf, cov, gram, gramx, wcol, zbuf,
    stz, stf, tgl, rs, tz, tgf, qf, gz, gf, gzs, gfull, sems, asem, lsem,
):
    f = lax.axis_index("frames")
    z = lax.axis_index("planes")
    comps, pixels = hf.shape
    total_frames = w0_ref.shape[0]
    fl = total_frames // nf
    tiles = pixels // TILE
    own = pl.ds(pl.multiple_of(f * fl, fl), fl)

    def over_frames(k, source, target, sems=sems):
        copies = []
        for d in range(1, nf):
            peer = lax.rem(f + d, nf)
            copies.append(
                pltpu.make_async_remote_copy(
                    src_ref=source(peer), dst_ref=target,
                    send_sem=sems.at[k, 0, d], recv_sem=sems.at[k, 1, d],
                    device_id=(peer, z), device_id_type=MESH,
                )
            )
        for copy in copies:
            copy.start()
        return copies

    def over_planes(k, source, target, sems=sems):
        copies = []
        for d in range(1, nz):
            peer = lax.rem(z + d, nz)
            copies.append(
                pltpu.make_async_remote_copy(
                    src_ref=source(peer), dst_ref=target,
                    send_sem=sems.at[k, 0, d], recv_sem=sems.at[k, 1, d],
                    device_id=(f, peer), device_id_type=MESH,
                )
            )
        for copy in copies:
            copy.start()
        return copies

    def wait(copies):
        for copy in copies:
            copy.wait()

    def load(source, target, k):
        copy = pltpu.make_async_copy(source, target, lsem.at[k])
        copy.start()
        return copy

    load_rec = load(rec_hbm, rec_ref, 1)
    load_tmpl = load(tmpl_hbm, tmpl_ref, 2)
    def part_of(device, c):
        return pl.ds(pl.multiple_of(device * pixels + c * TILE, TILE), TILE)

    peers = [(a, 0) for a in range(1, nf)] + [(0, b) for b in range(1, nz)]

    def peer_of(a, b):
        return (lax.rem(f + a, nf), lax.rem(z + b, nz))

    barrier = pltpu.get_barrier_semaphore()
    for a, b in peers:
        pl.semaphore_signal(barrier, inc=1, device_id=peer_of(a, b), device_id_type=MESH)

    load_rec.wait()
    load_tmpl.wait()
    load_h = load(h0_ref, hraw, 0)
    loads = [
        load(support_hbm, support_ref, 3),
        load(w0_hbm, w0_ref, 4),
        load(proj_hbm, proj_ref, 5),
    ]
    register(shifts_ref, rec_ref, tmpl_ref, payload_ref, stats_ref, reg_ref)
    pl.semaphore_wait(barrier, len(peers))

    stz[z] = stats_ref[...]
    plane_stats = over_planes(0, lambda peer: stats_ref, stz.at[z])
    pixel_copies = [
        over_frames(
            8 + c,
            lambda peer, c=c: payload_ref.at[:, part_of(peer, c)],
            rbuf.at[own, pl.ds(c * TILE, TILE)],
        )
        for c in range(tiles)
    ]

    for c in range(tiles):
        rbuf[own, c * TILE : (c + 1) * TILE] = payload_ref[:, part_of(f, c)]
    wait(plane_stats)
    summed = stz[0]
    for i in range(1, nz):
        summed = summed + stz[i]
    stf[f] = summed
    frame_stats = over_frames(1, lambda peer: stf.at[f], stf.at[f])

    load_h.wait()
    for copy in loads:
        copy.wait()
    gram[...] = jnp.zeros_like(gram)
    gramx[...] = jnp.zeros_like(gramx)
    first_tile = z * (pixel_count // TILE) + f * tiles

    def prepare(c, carry):
        hit = jnp.where(support_ref[...] == first_tile + c, 1.0, 0.0).astype(F32)
        row = jnp.max(hit, axis=0, keepdims=True)
        covered = jnp.broadcast_to(row, (LANES, comps)).T
        cov[c] = covered
        for j in range(TILE // LANES):
            columns = pl.ds(pl.multiple_of(c * TILE + j * LANES, LANES), LANES)
            lines = pl.ds(c * (TILE // LANES) + j, comps, stride=pixels // LANES)
            h = hraw[lines, :] * covered
            hf[:, columns] = h
            high, low = split(h)
            hhi[:, columns] = high
            hlo[:, columns] = low
        columns = pl.ds(pl.multiple_of(c * TILE, TILE), TILE)
        both = jnp.concatenate([hhi[:, columns], hlo[:, columns]], axis=0)
        product = dot1(both, hhi[:, columns], NT)
        gram[...] += product[:comps]
        gramx[...] += product[comps:]
        return carry

    lax.fori_loop(0, tiles, prepare, 0)
    gram[...] += gramx[...] + gramx[...].T
    block = comps // nz
    owned = pl.ds(pl.multiple_of(z * block, block), block)
    gram_scatter = over_planes(
        3, lambda peer: gram.at[pl.ds(pl.multiple_of(peer * block, block), block), :], gzs.at[z]
    )
    gzs[z] = gram[owned, :]
    w0 = w0_ref[...]
    tgl[...] = dot_rows(stack(split(w0)), *split(gram[...]))

    wait(frame_stats)
    template_energy = total(summed[2 * fl :, :])
    for s in range(nf):
        sums = stf[s]
        numerator = jnp.sum(sums[:fl], axis=1, keepdims=True)
        energy = jnp.sum(sums[fl : 2 * fl], axis=1, keepdims=True)
        weight = numerator / jnp.sqrt(energy * template_energy + epsilon)
        wcol[s * fl : (s + 1) * fl, :] = jnp.broadcast_to(weight, (fl, LANES))

    zbuf[...] = jnp.zeros_like(zbuf)
    for c in range(tiles):
        if c == tiles - 1:
            wait(gram_scatter)
            part = gzs[0]
            for i in range(1, nz):
                part = part + gzs[i]
            gfull[owned, :] = part
            gram_gather = over_planes(4, lambda peer: gfull.at[owned, :], gfull.at[owned, :])
        wait(pixel_copies[c])
        columns = pl.ds(c * TILE, TILE)
        series = rbuf[:, columns] * jnp.concatenate([wcol[...]] * (TILE // LANES), axis=1)
        rbuf[:, columns] = series
        zbuf[...] += dot_rows(stack(split(series)), hhi[:, columns], hlo[:, columns], NT)

    proj = deep_left(proj_ref[...])
    tgl[...] -= dot1(proj, deep_right(zbuf[...]))

    rs[f] = tgl[own, :]
    scatter = over_frames(
        2, lambda peer: tgl.at[pl.ds(pl.multiple_of(peer * fl, fl), fl), :], rs.at[f]
    )

    def detrend(c, carry):
        columns = pl.ds(pl.multiple_of(c * TILE, TILE), TILE)
        dbuf[:, columns] = dot1(proj, deep_right(rbuf[:, columns]))
        return carry

    lax.fori_loop(0, tiles, detrend, 0)
    wait(scatter)
    part = rs[0]
    for i in range(1, nf):
        part = part + rs[i]
    tz[z] = part
    wait(over_planes(5, lambda peer: tz.at[z], tz.at[z]))
    part = tz[0]
    for i in range(1, nz):
        part = part + tz[i]
    tgf[own, :] = part
    wait(over_frames(6, lambda peer: tgf.at[own, :], tgf.at[own, :]))

    grad = tgf[...]
    wait(gram_gather)
    bent = dot_rows(stack(split(grad)), *split(gfull[...]))
    qf[f] = fold(grad * bent)
    wait(over_frames(7, lambda peer: qf.at[f], qf.at[f]))
    curve = qf[0]
    for i in range(1, nf):
        curve = curve + qf[i]
    curve = total(curve)
    step = total(fold(grad * grad)) / (curve + epsilon)
    w1 = jnp.maximum(w0 - step * grad, 0.0)
    temporal_ref[...] = w1
    w1s = stack(split(w1))
    w1t = deep_left(w1.T)

    def gradient(c, carry):
        squares, curves = carry
        columns = pl.ds(pl.multiple_of(c * TILE, TILE), TILE)
        error = dot_rows(w1s, hhi[:, columns], hlo[:, columns]) - dbuf[:, columns]
        g = dot1(w1t, deep_right(error)) * jnp.concatenate([cov[c]] * (TILE // LANES), axis=1)
        gbuf[:, columns] = g
        bent = dot_rows(w1s, g.astype(BF16), None)
        return squares + fold(g * g), curves + fold(bent * bent)

    nothing = jnp.zeros((SUBS, LANES), F32)
    squares, curves = lax.fori_loop(0, tiles, gradient, (nothing, nothing))
    gz[z] = jnp.concatenate([squares, curves], axis=0)
    wait(over_planes(0, lambda peer: gz.at[z], gz.at[z], asem))
    sums = gz[0]
    for i in range(1, nz):
        sums = sums + gz[i]
    gf[f] = sums
    wait(over_frames(1, lambda peer: gf.at[f], gf.at[f], asem))
    sums = gf[0]
    for i in range(1, nf):
        sums = sums + gf[i]
    step = total(sums[:SUBS]) / (total(sums[SUBS:]) + epsilon)
    rows = comps // FINISH
    for b in range(FINISH):
        block = slice(b * rows, (b + 1) * rows)
        h_out[block, :] = jnp.maximum(hf[block, :] - step * gbuf[block, :], 0.0)


def finish_kernel(temporal_ref, h_ref, temporal_out, spatial_out, sems):
    comps, pixels = h_ref.shape
    lines = pixels // LANES
    first = pltpu.make_async_copy(temporal_ref, temporal_out, sems.at[lines])
    first.start()
    copies = [first]
    for j in range(lines):
        copy = pltpu.make_async_copy(
            h_ref.at[:, pl.ds(j * LANES, LANES)], spatial_out.at[:, j, :], sems.at[j]
        )
        copy.start()
        copies.append(copy)
    for copy in copies:
        copy.wait()


def body(nf, nz, recording, template, shifts, support, temporal_init, spatial_init):
    frames, planes, height, width = recording.shape
    comps = spatial_init.shape[0]
    pixels = spatial_init.shape[1] * spatial_init.shape[2]
    pixel_count = height * width
    total_frames = temporal_init.shape[0]
    tiles = pixels // TILE
    vmem = pl.BlockSpec(memory_space=pltpu.VMEM)
    hbm = pl.BlockSpec(memory_space=pltpu.HBM)
    smem = pl.BlockSpec(memory_space=pltpu.SMEM)
    count = max(nf, nz)
    temporal, refined = pl.pallas_call(
        functools.partial(main_kernel, nf, nz, pixel_count),
        out_shape=(
            jax.ShapeDtypeStruct((total_frames, comps), F32),
            jax.ShapeDtypeStruct((comps, pixels), F32),
        ),
        in_specs=[smem] + [hbm] * 6,
        out_specs=(vmem, vmem),
        scratch_shapes=[
            pltpu.VMEM((frames, height, width), F32),
            pltpu.VMEM((height, width), F32),
            pltpu.VMEM((support.shape[1], comps), jnp.int32),
            pltpu.VMEM((total_frames, total_frames), F32),
            pltpu.VMEM((total_frames, comps), F32),
            pltpu.VMEM((frames, pixel_count), F32),
            pltpu.VMEM((2 * frames + SUBS, LANES), F32),
            pltpu.VMEM((frames * height, width), F32),
            pltpu.VMEM((comps * pixels // LANES, LANES), F32),
            pltpu.VMEM((comps, pixels), BF16),
            pltpu.VMEM((comps, pixels), BF16),
            pltpu.VMEM((comps, pixels), F32),
            pltpu.VMEM((comps, pixels), F32),
            pltpu.VMEM((total_frames, pixels), F32),
            pltpu.VMEM((total_frames, pixels), F32),
            pltpu.VMEM((tiles, comps, LANES), F32),
            pltpu.VMEM((comps, comps), F32),
            pltpu.VMEM((comps, comps), F32),
            pltpu.VMEM((total_frames, LANES), F32),
            pltpu.VMEM((total_frames, comps), F32),
            pltpu.VMEM((nz, 2 * frames + SUBS, LANES), F32),
            pltpu.VMEM((nf, 2 * frames + SUBS, LANES), F32),
            pltpu.VMEM((total_frames, comps), F32),
            pltpu.VMEM((nf, frames, comps), F32),
            pltpu.VMEM((nz, frames, comps), F32),
            pltpu.VMEM((total_frames, comps), F32),
            pltpu.VMEM((nf, SUBS, LANES), F32),
            pltpu.VMEM((nz, 2 * SUBS, LANES), F32),
            pltpu.VMEM((nf, 2 * SUBS, LANES), F32),
            pltpu.VMEM((nz, comps // nz, comps), F32),
            pltpu.VMEM((comps, comps), F32),
            pltpu.SemaphoreType.DMA((8 + tiles, 2, count)),
            pltpu.SemaphoreType.DMA((2, 2, count)),
            pltpu.SemaphoreType.DMA((6,)),
        ],
        compiler_params=pltpu.CompilerParams(
            collective_id=0, has_side_effects=True, vmem_limit_bytes=VMEM_LIMIT
        ),
        name="factorize",
    )(
        shifts.reshape(frames, 2).T,
        recording.reshape(frames, height, width),
        template.reshape(height, width),
        support.T,
        jnp.asarray(trend_projection(total_frames, NTREND)),
        temporal_init,
        spatial_init.reshape(comps * pixels // LANES, LANES),
    )
    temporal, spatial = pl.pallas_call(
        finish_kernel,
        out_shape=(
            jax.ShapeDtypeStruct((total_frames, comps), F32),
            jax.ShapeDtypeStruct((comps, pixels // LANES, LANES), F32),
        ),
        in_specs=[vmem, vmem],
        out_specs=(hbm, hbm),
        scratch_shapes=[pltpu.SemaphoreType.DMA((pixels // LANES + 1,))],
        compiler_params=pltpu.CompilerParams(vmem_limit_bytes=1024 * 1024),
        name="finish",
    )(temporal, refined)
    return temporal, spatial.reshape(spatial_init.shape)


def solution(mesh):
    placed = (
        P("frames", "planes", None, None),
        P("planes", None, None),
        P("frames", "planes", None),
        P(),
        P(),
        P(None, "planes", "frames"),
    )
    return jax.shard_map(
        functools.partial(body, mesh.shape["frames"], mesh.shape["planes"]),
        mesh=mesh,
        in_specs=placed,
        out_specs=(P(), P(None, "planes", "frames")),
        check_vma=False,
    )
```

```python
import functools

import jax
import jax.numpy as jnp
import numpy as np
from jax import lax
from jax.experimental import pallas as pl
from jax.experimental.pallas import tpu as pltpu
from jax.sharding import PartitionSpec as P

TILE = 1024
NTREND = 16
LANES = 128
SUBS = 8
FINISH = 8
VMEM_LIMIT = 60 * 1000 * 1000
MESH = pl.DeviceIdType.MESH
F32 = jnp.float32
BF16 = jnp.bfloat16

epsilon = 1e-06

NN = (((1,), (0,)), ((), ()))
NT = (((1,), (1,)), ((), ()))


def trend_projection(frame_count, basis_order):
    times = np.arange(frame_count) + 0.5
    orders = np.arange(basis_order)
    scales = np.where(orders == 0, np.sqrt(1.0 / frame_count), np.sqrt(2.0 / frame_count))
    basis = np.cos(np.pi * times[:, None] * orders[None, :] / frame_count) * scales[None, :]
    return (np.eye(frame_count) - basis @ basis.T).astype(np.float32)


def split(x):
    high = x.astype(BF16)
    return high, (x - high.astype(F32)).astype(BF16)


def dot1(a, b, dims=NN):
    return lax.dot_general(a, b, dims, preferred_element_type=F32)


def stack(a):
    return jnp.concatenate(a, axis=0)


def dot_rows(stacked, high, low, dims=NN):
    rows = stacked.shape[0] // 2
    first = dot1(stacked, high, dims)
    first = first[:rows] + first[rows:]
    if low is None:
        return first
    return first + dot1(stacked[:rows], low, dims)


def deep_left(x):
    high, low = split(x)
    return jnp.concatenate([high, low, high], axis=1)


def deep_right(x):
    high, low = split(x)
    return jnp.concatenate([high, high, low], axis=0)


def fold(x):
    rows, columns = x.shape
    line = x[:, :LANES]
    for j in range(1, columns // LANES):
        line = line + x[:, j * LANES : (j + 1) * LANES]
    return jnp.sum(line.reshape(rows // SUBS, SUBS, LANES), axis=0)


def total(x):
    return jnp.sum(jnp.sum(x, axis=0, keepdims=True), axis=1, keepdims=True)


def register(shifts_ref, rec_ref, tmpl_ref, payload_ref, stats_ref, reg_ref):
    frames, height, width = rec_ref.shape
    tmpl = tmpl_ref[...]
    for f in range(frames):
        x = rec_ref[f]
        across = lax.rem(shifts_ref[1, f] + width, width)
        down = lax.rem(shifts_ref[0, f] + height, height)
        y = pltpu.roll(pltpu.roll(x, across, 1), down, 0)
        reg_ref[f * height : (f + 1) * height, :] = y
        stats_ref[f : f + 1, :] = jnp.sum(y * tmpl, axis=0, keepdims=True)
        stats_ref[frames + f : frames + f + 1, :] = jnp.sum(x * x, axis=0, keepdims=True)
    stats_ref[2 * frames :, :] = fold(tmpl * tmpl)
    for r in range(height):
        payload_ref[:, r * width : (r + 1) * width] = reg_ref[pl.ds(r, frames, stride=height), :]


def main_kernel(
    nf, nz, pixel_count,
    shifts_ref, rec_hbm, tmpl_hbm, support_hbm, proj_hbm, w0_hbm, h0_ref,
    temporal_ref, h_out,
    rec_ref, tmpl_ref, support_ref, proj_ref, w0_ref, payload_ref, stats_ref, reg_ref,
    hraw, hhi, hlo, hf, gbuf, rbuf, dbuf, cov, gram, gramx, wcol, zbuf,
    stz, stf, tgl, rs, tz, tgf, qf, gz, gf, gzs, gfull, sems, asem, lsem,
):
    f = lax.axis_index("frames")
    z = lax.axis_index("planes")
    comps, pixels = hf.shape
    total_frames = w0_ref.shape[0]
    fl = total_frames // nf
    tiles = pixels // TILE
    own = pl.ds(pl.multiple_of(f * fl, fl), fl)

    def over_frames(k, source, target, sems=sems):
        copies = []
        for d in range(1, nf):
            peer = lax.rem(f + d, nf)
            copies.append(
                pltpu.make_async_remote_copy(
                    src_ref=source(peer), dst_ref=target,
                    send_sem=sems.at[k, 0, d], recv_sem=sems.at[k, 1, d],
                    device_id=(peer, z), device_id_type=MESH,
                )
            )
        for copy in copies:
            copy.start()
        return copies

    def over_planes(k, source, target, sems=sems):
        copies = []
        for d in range(1, nz):
            peer = lax.rem(z + d, nz)
            copies.append(
                pltpu.make_async_remote_copy(
                    src_ref=source(peer), dst_ref=target,
                    send_sem=sems.at[k, 0, d], recv_sem=sems.at[k, 1, d],
                    device_id=(f, peer), device_id_type=MESH,
                )
            )
        for copy in copies:
            copy.start()
        return copies

    def wait(copies):
        for copy in copies:
            copy.wait()

    def load(source, target, k):
        copy = pltpu.make_async_copy(source, target, lsem.at[k])
        copy.start()
        return copy

    load_rec = load(rec_hbm, rec_ref, 1)
    load_tmpl = load(tmpl_hbm, tmpl_ref, 2)
    def part_of(device, c):
        return pl.ds(pl.multiple_of(device * pixels + c * TILE, TILE), TILE)

    peers = [(a, 0) for a in range(1, nf)] + [(0, b) for b in range(1, nz)]

    def peer_of(a, b):
        return (lax.rem(f + a, nf), lax.rem(z + b, nz))

    barrier = pltpu.get_barrier_semaphore()
    for a, b in peers:
        pl.semaphore_signal(barrier, inc=1, device_id=peer_of(a, b), device_id_type=MESH)

    load_rec.wait()
    load_tmpl.wait()
    load_h = load(h0_ref, hraw, 0)
    loads = [
        load(support_hbm, support_ref, 3),
        load(w0_hbm, w0_ref, 4),
        load(proj_hbm, proj_ref, 5),
    ]
    register(shifts_ref, rec_ref, tmpl_ref, payload_ref, stats_ref, reg_ref)
    pl.semaphore_wait(barrier, len(peers))

    stz[z] = stats_ref[...]
    plane_stats = over_planes(0, lambda peer: stats_ref, stz.at[z])
    pixel_copies = [
        over_frames(
            8 + c,
            lambda peer, c=c: payload_ref.at[:, part_of(peer, c)],
            rbuf.at[own, pl.ds(c * TILE, TILE)],
        )
        for c in range(tiles)
    ]

    for c in range(tiles):
        rbuf[own, c * TILE : (c + 1) * TILE] = payload_ref[:, part_of(f, c)]
    wait(plane_stats)
    summed = stz[0]
    for i in range(1, nz):
        summed = summed + stz[i]
    stf[f] = summed
    frame_stats = over_frames(1, lambda peer: stf.at[f], stf.at[f])

    load_h.wait()
    for copy in loads:
        copy.wait()
    gram[...] = jnp.zeros_like(gram)
    gramx[...] = jnp.zeros_like(gramx)
    first_tile = z * (pixel_count // TILE) + f * tiles

    def prepare(c, carry):
        hit = jnp.where(support_ref[...] == first_tile + c, 1.0, 0.0).astype(F32)
        row = jnp.max(hit, axis=0, keepdims=True)
        covered = jnp.broadcast_to(row, (LANES, comps)).T
        cov[c] = covered
        for j in range(TILE // LANES):
            columns = pl.ds(pl.multiple_of(c * TILE + j * LANES, LANES), LANES)
            lines = pl.ds(c * (TILE // LANES) + j, comps, stride=pixels // LANES)
            h = hraw[lines, :] * covered
            hf[:, columns] = h
            high, low = split(h)
            hhi[:, columns] = high
            hlo[:, columns] = low
        columns = pl.ds(pl.multiple_of(c * TILE, TILE), TILE)
        both = jnp.concatenate([hhi[:, columns], hlo[:, columns]], axis=0)
        product = dot1(both, hhi[:, columns], NT)
        gram[...] += product[:comps]
        gramx[...] += product[comps:]
        return carry

    lax.fori_loop(0, tiles, prepare, 0)
    gram[...] += gramx[...] + gramx[...].T
    block = comps // nz
    owned = pl.ds(pl.multiple_of(z * block, block), block)
    gram_scatter = over_planes(
        3, lambda peer: gram.at[pl.ds(pl.multiple_of(peer * block, block), block), :], gzs.at[z]
    )
    gzs[z] = gram[owned, :]
    w0 = w0_ref[...]
    tgl[...] = dot_rows(stack(split(w0)), *split(gram[...]))

    wait(frame_stats)
    template_energy = total(summed[2 * fl :, :])
    for s in range(nf):
        sums = stf[s]
        numerator = jnp.sum(sums[:fl], axis=1, keepdims=True)
        energy = jnp.sum(sums[fl : 2 * fl], axis=1, keepdims=True)
        weight = numerator / jnp.sqrt(energy * template_energy + epsilon)
        wcol[s * fl : (s + 1) * fl, :] = jnp.broadcast_to(weight, (fl, LANES))

    zbuf[...] = jnp.zeros_like(zbuf)
    for c in range(tiles):
        if c == max(tiles - 2, 0):
            wait(gram_scatter)
            part = gzs[0]
            for i in range(1, nz):
                part = part + gzs[i]
            gfull[owned, :] = part
            gram_gather = over_planes(4, lambda peer: gfull.at[owned, :], gfull.at[owned, :])
        wait(pixel_copies[c])
        columns = pl.ds(c * TILE, TILE)
        series = rbuf[:, columns] * jnp.concatenate([wcol[...]] * (TILE // LANES), axis=1)
        rbuf[:, columns] = series
        zbuf[...] += dot_rows(stack(split(series)), hhi[:, columns], hlo[:, columns], NT)

    proj = deep_left(proj_ref[...])
    tgl[...] -= dot1(proj, deep_right(zbuf[...]))

    rs[f] = tgl[own, :]
    scatter = over_frames(
        2, lambda peer: tgl.at[pl.ds(pl.multiple_of(peer * fl, fl), fl), :], rs.at[f]
    )

    def detrend(c, carry):
        columns = pl.ds(pl.multiple_of(c * TILE, TILE), TILE)
        dbuf[:, columns] = dot1(proj, deep_right(rbuf[:, columns]))
        return carry

    lax.fori_loop(0, tiles, detrend, 0)
    wait(scatter)
    part = rs[0]
    for i in range(1, nf):
        part = part + rs[i]
    tz[z] = part
    wait(over_planes(5, lambda peer: tz.at[z], tz.at[z]))
    part = tz[0]
    for i in range(1, nz):
        part = part + tz[i]
    tgf[own, :] = part
    wait(over_frames(6, lambda peer: tgf.at[own, :], tgf.at[own, :]))

    grad = tgf[...]
    wait(gram_gather)
    bent = dot_rows(stack(split(grad)), *split(gfull[...]))
    qf[f] = fold(grad * bent)
    wait(over_frames(7, lambda peer: qf.at[f], qf.at[f]))
    curve = qf[0]
    for i in range(1, nf):
        curve = curve + qf[i]
    curve = total(curve)
    step = total(fold(grad * grad)) / (curve + epsilon)
    w1 = jnp.maximum(w0 - step * grad, 0.0)
    temporal_ref[...] = w1
    w1s = stack(split(w1))
    w1t = deep_left(w1.T)

    def gradient(c, carry):
        squares, curves = carry
        columns = pl.ds(pl.multiple_of(c * TILE, TILE), TILE)
        error = dot_rows(w1s, hhi[:, columns], hlo[:, columns]) - dbuf[:, columns]
        g = dot1(w1t, deep_right(error)) * jnp.concatenate([cov[c]] * (TILE // LANES), axis=1)
        gbuf[:, columns] = g
        bent = dot_rows(w1s, g.astype(BF16), None)
        return squares + fold(g * g), curves + fold(bent * bent)

    nothing = jnp.zeros((SUBS, LANES), F32)
    squares, curves = lax.fori_loop(0, tiles, gradient, (nothing, nothing))
    gz[z] = jnp.concatenate([squares, curves], axis=0)
    wait(over_planes(0, lambda peer: gz.at[z], gz.at[z], asem))
    sums = gz[0]
    for i in range(1, nz):
        sums = sums + gz[i]
    gf[f] = sums
    wait(over_frames(1, lambda peer: gf.at[f], gf.at[f], asem))
    sums = gf[0]
    for i in range(1, nf):
        sums = sums + gf[i]
    step = total(sums[:SUBS]) / (total(sums[SUBS:]) + epsilon)
    rows = comps // FINISH
    for b in range(FINISH):
        block = slice(b * rows, (b + 1) * rows)
        h_out[block, :] = jnp.maximum(hf[block, :] - step * gbuf[block, :], 0.0)


def finish_kernel(temporal_ref, h_ref, temporal_out, spatial_out, sems):
    comps, pixels = h_ref.shape
    lines = pixels // LANES
    first = pltpu.make_async_copy(temporal_ref, temporal_out, sems.at[lines])
    first.start()
    copies = [first]
    for j in range(lines):
        copy = pltpu.make_async_copy(
            h_ref.at[:, pl.ds(j * LANES, LANES)], spatial_out.at[:, j, :], sems.at[j]
        )
        copy.start()
        copies.append(copy)
    for copy in copies:
        copy.wait()


def body(nf, nz, recording, template, shifts, support, temporal_init, spatial_init):
    frames, planes, height, width = recording.shape
    comps = spatial_init.shape[0]
    pixels = spatial_init.shape[1] * spatial_init.shape[2]
    pixel_count = height * width
    total_frames = temporal_init.shape[0]
    tiles = pixels // TILE
    vmem = pl.BlockSpec(memory_space=pltpu.VMEM)
    hbm = pl.BlockSpec(memory_space=pltpu.HBM)
    smem = pl.BlockSpec(memory_space=pltpu.SMEM)
    count = max(nf, nz)
    temporal, refined = pl.pallas_call(
        functools.partial(main_kernel, nf, nz, pixel_count),
        out_shape=(
            jax.ShapeDtypeStruct((total_frames, comps), F32),
            jax.ShapeDtypeStruct((comps, pixels), F32),
        ),
        in_specs=[smem] + [hbm] * 6,
        out_specs=(vmem, vmem),
        scratch_shapes=[
            pltpu.VMEM((frames, height, width), F32),
            pltpu.VMEM((height, width), F32),
            pltpu.VMEM((support.shape[1], comps), jnp.int32),
            pltpu.VMEM((total_frames, total_frames), F32),
            pltpu.VMEM((total_frames, comps), F32),
            pltpu.VMEM((frames, pixel_count), F32),
            pltpu.VMEM((2 * frames + SUBS, LANES), F32),
            pltpu.VMEM((frames * height, width), F32),
            pltpu.VMEM((comps * pixels // LANES, LANES), F32),
            pltpu.VMEM((comps, pixels), BF16),
            pltpu.VMEM((comps, pixels), BF16),
            pltpu.VMEM((comps, pixels), F32),
            pltpu.VMEM((comps, pixels), F32),
            pltpu.VMEM((total_frames, pixels), F32),
            pltpu.VMEM((total_frames, pixels), F32),
            pltpu.VMEM((tiles, comps, LANES), F32),
            pltpu.VMEM((comps, comps), F32),
            pltpu.VMEM((comps, comps), F32),
            pltpu.VMEM((total_frames, LANES), F32),
            pltpu.VMEM((total_frames, comps), F32),
            pltpu.VMEM((nz, 2 * frames + SUBS, LANES), F32),
            pltpu.VMEM((nf, 2 * frames + SUBS, LANES), F32),
            pltpu.VMEM((total_frames, comps), F32),
            pltpu.VMEM((nf, frames, comps), F32),
            pltpu.VMEM((nz, frames, comps), F32),
            pltpu.VMEM((total_frames, comps), F32),
            pltpu.VMEM((nf, SUBS, LANES), F32),
            pltpu.VMEM((nz, 2 * SUBS, LANES), F32),
            pltpu.VMEM((nf, 2 * SUBS, LANES), F32),
            pltpu.VMEM((nz, comps // nz, comps), F32),
            pltpu.VMEM((comps, comps), F32),
            pltpu.SemaphoreType.DMA((8 + tiles, 2, count)),
            pltpu.SemaphoreType.DMA((2, 2, count)),
            pltpu.SemaphoreType.DMA((6,)),
        ],
        compiler_params=pltpu.CompilerParams(
            collective_id=0, has_side_effects=True, vmem_limit_bytes=VMEM_LIMIT
        ),
        name="factorize",
    )(
        shifts.reshape(frames, 2).T,
        recording.reshape(frames, height, width),
        template.reshape(height, width),
        support.T,
        jnp.asarray(trend_projection(total_frames, NTREND)),
        temporal_init,
        spatial_init.reshape(comps * pixels // LANES, LANES),
    )
    temporal, spatial = pl.pallas_call(
        finish_kernel,
        out_shape=(
            jax.ShapeDtypeStruct((total_frames, comps), F32),
            jax.ShapeDtypeStruct((comps, pixels // LANES, LANES), F32),
        ),
        in_specs=[vmem, vmem],
        out_specs=(hbm, hbm),
        scratch_shapes=[pltpu.SemaphoreType.DMA((pixels // LANES + 1,))],
        compiler_params=pltpu.CompilerParams(vmem_limit_bytes=1024 * 1024),
        name="finish",
    )(temporal, refined)
    return temporal, spatial.reshape(spatial_init.shape)


def solution(mesh):
    placed = (
        P("frames", "planes", None, None),
        P("planes", None, None),
        P("frames", "planes", None),
        P(),
        P(),
        P(None, "planes", "frames"),
    )
    return jax.shard_map(
        functools.partial(body, mesh.shape["frames"], mesh.shape["planes"]),
        mesh=mesh,
        in_specs=placed,
        out_specs=(P(), P(None, "planes", "frames")),
        check_vma=False,
    )
```
